32 devices in a mesh: dp: 4 (over y, x), mp: 8 (over z, core).
Axes of the slice: x: 2, y: 2, z: 4, core: 2. Of those that a mesh axis runs over, the one named last changes fastest.
Arguments:
- train_acts: bfloat16 [512, 4096], P('dp', 'mp'), may hold values from -6 to 6
- train_grads: bfloat16 [512, 7168], P('dp', 'mp'), may hold values from -0.75 to 0.75
- query_acts: bfloat16 [1024, 4096], P('dp', 'mp'), may hold values from -6 to 6
- query_grads: bfloat16 [1024, 7168], P('dp', 'mp'), may hold values from -0.75 to 0.75
- basis_in: bfloat16 [4096, 4096], P('mp'), may hold values from -0.125 to 0.125
- basis_out: bfloat16 [7168, 7168], P('mp'), may hold values from -0.09375 to 0.09375
- eigvals: bfloat16 [4096, 7168], P(None, 'mp'), may hold values from 0.25 to 4
Outputs:
- scores: float32 [16, 8], P(None, 'dp')
- energies: float32 [8], P('dp')
The draws below stay inside these ranges and needn't reach their ends.
All inputs are finite; a program needn't handle non-finite values.
Results may differ from the reference program's by a relative error of at most 0.0048.
Values may be sent and summed in bfloat16 or wider, within the bound.
No kernel may reach another device: no remote copies, remote signals or barrier semaphores. Data moves between devices by JAX's collectives and lax.ppermute only.
A program may use at most 128 MiB of HBM per device.

```python
import math
import jax
import jax.numpy as jnp
from jax import lax

D = 4096
H = 7168
SEQ = 64
QSEQ = 16
TRAIN = 8
N_MP = 8


def strengthened(drawn, rng, source, target, parts, factor):
    def block_of(dim):
        return (jnp.arange(drawn.shape[dim]) // (drawn.shape[dim] // parts)).reshape((-1,) + (1,) * (drawn.ndim - 1 - dim))

    one_side = jax.random.permutation(rng, parts)[block_of(target)]
    second = (block_of(target) + parts // 2) % parts
    return jnp.where((block_of(source) == one_side) | (block_of(source) == second), factor * drawn, drawn)


def block_scale(rng, shape, cuts, smallest, high):
    loudness, own = 1.0, jax.random.fold_in(rng, 6)
    for axis_at, parts in cuts:
        heights = jnp.exp(jax.random.uniform(jax.random.fold_in(own, axis_at), (parts,), jnp.float32, smallest / len(cuts), high / len(cuts)))
        loudness = loudness * jnp.repeat(heights, shape[axis_at] // parts).reshape([-1 if axis == axis_at else 1 for axis in range(len(shape))])
    return loudness


def centred(key, extent, spread, bound, split=(), held_as=jnp.bfloat16):
    loudness = block_scale(key, extent, split, -0.22, 0.18) if split else 1.0
    values = jax.random.normal(key, extent, jnp.float32) * spread * loudness
    return jnp.minimum(jnp.maximum(values, -bound), bound).astype(held_as)


def heavy_noise(rng, dims, width, limit, split, heavy, kind=jnp.bfloat16):
    entries = width * jax.random.normal(rng, dims, jnp.float32)
    if split:
        entries = entries * block_scale(rng, dims, split, -0.22, 0.18)
    return jnp.clip(strengthened(entries, jax.random.fold_in(rng, 3), *heavy), -limit, limit).astype(kind)


def setup_inputs(seed: int = 0) -> dict:
    seeds = jax.random.split(jax.random.key(seed), 8)
    return {
        "train_acts": centred(seeds[0], (TRAIN * SEQ, D), 1.0, 6.0, ((0, 4), (1, 8))),
        "train_grads": centred(seeds[1], (TRAIN * SEQ, H), 0.125, 0.75, ((0, 4), (1, 8))),
        "query_acts": centred(seeds[2], (QSEQ * SEQ, D), 1.0, 6.0, ((0, 4), (1, 8))),
        "query_grads": centred(seeds[3], (QSEQ * SEQ, H), 0.125, 0.75, ((0, 4), (1, 8))),
        "basis_in": heavy_noise(seeds[4], (D, D), D ** -0.5, 0.125, ((0, 8),), (0, 1, 8, 2.0)),
        "basis_out": heavy_noise(seeds[5], (H, H), H ** -0.5, 0.09375, ((0, 8),), (0, 1, 8, 2.0)),
        "eigvals": jnp.clip(jnp.exp(math.log(4.0) - 2.7725887 * jax.random.uniform(seeds[6], (D, H), jnp.float32) ** block_scale(seeds[6], (D, H), ((1, 8),), -0.2, 0.2)), 0.25, 4.0).astype(jnp.bfloat16),
    }


damping = 0.1

def reference(train_acts, train_grads, query_acts, query_grads, basis_in, basis_out, eigvals):
    train_rot_a = jnp.dot(train_acts, basis_in, preferred_element_type=jnp.float32).astype(jnp.bfloat16).reshape(TRAIN, SEQ, D)
    query_rot_a = jnp.dot(query_acts, basis_in, preferred_element_type=jnp.float32).astype(jnp.bfloat16).reshape(QSEQ, SEQ, D)
    train_rot_g = jnp.dot(train_grads, basis_out, preferred_element_type=jnp.float32).astype(jnp.bfloat16).reshape(TRAIN, SEQ, H)
    query_rot_g = jnp.dot(query_grads, basis_out, preferred_element_type=jnp.float32).astype(jnp.bfloat16).reshape(QSEQ, SEQ, H)
    block_width = H // N_MP
    train_wide = train_rot_a.astype(jnp.float32)
    query_wide = query_rot_a.astype(jnp.float32)

    def one_block(block_index):
        offset = block_index * block_width
        train_part = lax.dynamic_slice_in_dim(train_rot_g, offset, block_width, 2).astype(jnp.float32)
        query_part = lax.dynamic_slice_in_dim(query_rot_g, offset, block_width, 2).astype(jnp.float32)
        shifted = lax.dynamic_slice_in_dim(eigvals, offset, block_width, 1).astype(jnp.float32) + damping
        train_outer = jnp.einsum('nsi,nsj->nij', train_wide, train_part)
        rounded = lax.optimization_barrier((train_outer / shifted).astype(jnp.bfloat16))
        scaled = rounded.astype(jnp.float32)
        query_outer = jnp.einsum('qsi,qsj->qij', query_wide, query_part)
        block_scores = jnp.einsum('qij,nij->qn', query_outer, scaled, precision=lax.Precision.HIGHEST)
        energy = lax.optimization_barrier(jnp.sum(train_outer * train_outer, axis=(1, 2)))
        return (block_scores, energy)
    pieces = lax.map(one_block, jnp.arange(N_MP, dtype=jnp.int32))
    scores = lax.optimization_barrier(jnp.sum(pieces[0], axis=0)) * (1.0 / math.sqrt(D * H))
    energies = lax.optimization_barrier(jnp.sum(pieces[1], axis=0)) / (D * H)
    return (scores, energies)
```

```python
import functools
import math

import jax
import jax.numpy as jnp
from jax import lax
from jax.experimental import pallas as pl
from jax.experimental.pallas import tpu as pltpu
from jax.sharding import PartitionSpec as P

SEQ = 64
LANES = 128

damping = 0.1

ACTS_MAX, BASIS_IN_MAX = 6.0, 0.125
GRADS_MAX, BASIS_OUT_MAX = 0.75, 0.09375

Q_CHUNKS = 2


def gain_of(bound):
    return 2.0 ** math.floor(math.log2(65000.0**2 / bound))


def encode(value, gain):
    root = jnp.sqrt(jnp.abs(value) * gain)
    return jnp.where(value < 0, -root, root).astype(jnp.float16)


def decode(coded, gain):
    root = coded.astype(jnp.float32)
    return root * jnp.abs(root) * (1.0 / gain)


def reversed_bits(p, bits):
    out = 0
    for b in range(bits):
        out |= ((p >> b) & 1) << (bits - 1 - b)
    return out


def swap(x, axis, size, mask):
    return lax.ppermute(x, axis, [(k, k ^ mask) for k in range(size)])


def rotate_kernel(n_parts, cuts, order_ref, *refs):
    x_ref, parts, outs = refs[0], refs[1 : 1 + n_parts], refs[1 + n_parts :]
    basis = jnp.concatenate([part[...] for part in parts], axis=1) if n_parts > 1 else parts[0][...]
    value = jnp.dot(x_ref[...], basis, preferred_element_type=jnp.float32)
    for out, (start, rows) in zip(outs, cuts):
        out[0] = value[start : start + rows]


def rotate(x, basis, me, order_mp, order_dp, cuts):
    rows, feats = x.shape
    n_mp, n_dp = len(order_mp), len(order_dp[1])
    width = basis.shape[1] // n_mp
    cell = width // n_dp
    blocks = me ^ jnp.array(order_mp, jnp.int32)
    cells = order_dp[0] ^ jnp.array(order_dp[1], jnp.int32)
    if cell % LANES:
        chosen = jnp.take(jnp.take(basis.reshape(feats, n_mp, n_dp, cell), blocks, axis=1), cells, axis=2)
        value = jnp.einsum("rf,fpec->prec", x, chosen, preferred_element_type=jnp.float32)
        value = value.reshape(n_mp, rows, width)
        return [value[:, start : start + size] for start, size in cuts]
    order = jnp.concatenate([blocks, cells])

    def part_map(e, p, order_ref):
        return (0, order_ref[p] * n_dp + order_ref[n_mp + e])

    return pl.pallas_call(
        functools.partial(rotate_kernel, n_dp, tuple(cuts)),
        grid_spec=pltpu.PrefetchScalarGridSpec(
            num_scalar_prefetch=1,
            grid=(n_mp,),
            in_specs=[pl.BlockSpec((rows, feats), lambda p, order_ref: (0, 0))]
            + [pl.BlockSpec((feats, cell), functools.partial(part_map, e)) for e in range(n_dp)],
            out_specs=[pl.BlockSpec((1, size, width), lambda p, order_ref: (p, 0, 0)) for _, size in cuts],
        ),
        out_shape=[jax.ShapeDtypeStruct((n_mp, size, width), jnp.float32) for _, size in cuts],
        name="rotate",
    )(order, x, *([basis] * n_dp))


def reduce_over_mp(parts, gain, n_mp):
    have = parts
    bit = 1
    while bit < n_mp:
        half = have.shape[0] // 2
        got = swap(encode(have[half:], gain), "mp", n_mp, bit)
        have = have[:half] + decode(got, gain)
        bit *= 2
    return have[0].astype(jnp.bfloat16)


def scale_kernel(n_dp, seqs, order_ref, low_ref, high_ref, *refs):
    g_refs, eig_ref, scaled_ref, energy_ref = refs[:n_dp], refs[n_dp], refs[n_dp + 1], refs[n_dp + 2]
    p, half = pl.program_id(0), pl.num_programs(0) // 2

    @pl.when(p == 0)
    def _():
        energy_ref[...] = jnp.zeros_like(energy_ref)

    inverse = 1.0 / (eig_ref[...].astype(jnp.float32) + damping)
    for e in range(n_dp):
        for s in range(seqs):
            span = slice(s * SEQ, (s + 1) * SEQ)
            a = jnp.where(p < half, low_ref[0, e, span, :], high_ref[0, e, span, :])
            outer = lax.dot_general(a, g_refs[e][span, :], (((0,), (0,)), ((), ())), preferred_element_type=jnp.float32)
            n = order_ref[e] * seqs + s
            scaled_ref[n] = (outer * inverse).astype(jnp.bfloat16)
            squares = jnp.sum((outer * outer).reshape(-1, 8, outer.shape[1]), axis=0)
            energy_ref[n] += squares


def scale(low, high, train_g, eig_rows, n_mp, order):
    n_dp, rows, cell = low.shape[1:]
    width = train_g[0].shape[1]
    seqs = rows // SEQ
    total = n_dp * seqs
    half = n_mp // 2
    eig, eig_map = eig_rows
    return pl.pallas_call(
        functools.partial(scale_kernel, n_dp, seqs),
        grid_spec=pltpu.PrefetchScalarGridSpec(
            num_scalar_prefetch=1,
            grid=(n_mp,),
            in_specs=[
                pl.BlockSpec((1, n_dp, rows, cell), lambda p, o: (jnp.minimum(p, half - 1), 0, 0, 0)),
                pl.BlockSpec((1, n_dp, rows, cell), lambda p, o: (jnp.maximum(p - half, 0), 0, 0, 0)),
            ]
            + [pl.BlockSpec((rows, width), lambda p, o: (0, 0)) for _ in range(n_dp)]
            + [pl.BlockSpec((cell, width), eig_map)],
            out_specs=[
                pl.BlockSpec((total, cell, width), lambda p, o: (0, p, 0)),
                pl.BlockSpec((total, 8, width), lambda p, o: (0, 0, 0)),
            ],
        ),
        out_shape=[
            jax.ShapeDtypeStruct((total, n_mp * cell, width), jnp.bfloat16),
            jax.ShapeDtypeStruct((total, 8, width), jnp.float32),
        ],
        name="scale",
    )(order, low, high, *train_g, eig)


def score_kernel(n_dp, seqs, order_ref, low_ref, high_ref, *refs):
    g_refs, scaled_ref, out_ref, a_scr, g_scr = refs[:n_dp], refs[n_dp], refs[n_dp + 1], refs[n_dp + 2], refs[n_dp + 3]
    half, _, rows, cell = low_ref.shape

    @pl.when(pl.program_id(0) == 0)
    def _():
        for e in range(n_dp):
            at = pl.ds(pl.multiple_of(order_ref[e] * rows, rows), rows)
            for p in range(half):
                a_scr[at, p * cell : (p + 1) * cell] = low_ref[p, e]
                a_scr[at, (half + p) * cell : (half + p + 1) * cell] = high_ref[p, e]
            g_scr[at, :] = g_refs[e][...]

    tokens = a_scr.shape[0]
    tile = math.gcd(tokens, 256)
    for t in range(tokens // tile):
        span = slice(t * tile, (t + 1) * tile)
        applied = jnp.dot(a_scr[span, :], scaled_ref[0], preferred_element_type=jnp.float32)
        product = applied * g_scr[span, :].astype(jnp.float32)
        for q in range(tile // SEQ):
            out_ref[0, pl.ds(t * (tile // SEQ) + q, 1), :] = jnp.sum(product[q * SEQ : (q + 1) * SEQ], axis=0, keepdims=True)


def score(low, high, query_g, scaled, chunk, rows, order):
    half, n_dp, _, cell = low.shape
    total, depth, width = scaled.shape
    seqs = rows // SEQ
    return pl.pallas_call(
        functools.partial(score_kernel, n_dp, seqs),
        grid_spec=pltpu.PrefetchScalarGridSpec(
            num_scalar_prefetch=1,
            grid=(total,),
            in_specs=[pl.BlockSpec((half, n_dp, rows, cell), lambda n, o: (0, 0, chunk, 0))] * 2
            + [pl.BlockSpec((rows, width), lambda n, o: (0, 0)) for _ in range(n_dp)]
            + [pl.BlockSpec((1, depth, width), lambda n, o: (n, 0, 0))],
            out_specs=pl.BlockSpec((1, n_dp * seqs, width), lambda n, o: (n, 0, 0)),
            scratch_shapes=[
                pltpu.VMEM((n_dp * rows, depth), jnp.bfloat16),
                pltpu.VMEM((n_dp * rows, width), jnp.bfloat16),
            ],
        ),
        out_shape=jax.ShapeDtypeStruct((total, n_dp * seqs, width), jnp.float32),
        name="score",
    )(order, low, high, *query_g, scaled)


def on_device(n_dp, n_mp, train_acts, train_grads, query_acts, query_grads, basis_in, basis_out, eigvals):
    me, home = lax.axis_index("mp"), lax.axis_index("dp")
    bits = n_mp.bit_length() - 1
    order_mp = [reversed_bits(p, bits) for p in range(n_mp)]
    order_e = list(range(n_dp))
    n_train, n_query = train_acts.shape[0], query_acts.shape[0]
    features, hidden = basis_in.shape[1], basis_out.shape[1]
    cell = features // (n_mp * n_dp)
    width = hidden // n_mp
    gain_a = gain_of(features * ACTS_MAX * BASIS_IN_MAX)
    gain_g = gain_of(hidden * GRADS_MAX * BASIS_OUT_MAX)
    chunks = Q_CHUNKS if n_query % (Q_CHUNKS * SEQ) == 0 else 1
    rows_q = n_query // chunks
    natural = home ^ jnp.arange(n_dp, dtype=jnp.int32)

    acts = jnp.concatenate([train_acts, query_acts], axis=0)
    grads = jnp.concatenate([train_grads, query_grads], axis=0)

    cuts_a = [(0, n_train), (n_train, n_query)]
    parts_a = rotate(acts, basis_in, me, order_mp, (home, order_e), cuts_a)
    cuts_g = [(0, n_train)] + [(n_train + k * rows_q, rows_q) for k in range(chunks)]
    parts_g = rotate(grads, basis_out, me, order_mp, (0, [0]), cuts_g)

    def gathered_a(parts):
        mine = reduce_over_mp(parts, gain_a, n_mp)
        pieces = [mine[:, e * cell : (e + 1) * cell] for e in range(n_dp)]
        pieces = [pieces[0]] + [swap(pieces[e], "dp", n_dp, e) for e in range(1, n_dp)]
        have = jnp.stack(pieces)[None]
        bit = n_mp // 2
        while bit > 1:
            have = jnp.concatenate([have, swap(have, "mp", n_mp, bit)], axis=0)
            bit //= 2
        return have, swap(have, "mp", n_mp, 1)

    def gathered_g(parts):
        mine = reduce_over_mp(parts, gain_g, n_mp)
        return [mine] + [swap(mine, "dp", n_dp, e) for e in range(1, n_dp)]

    train_a = gathered_a(parts_a[0])
    train_g = gathered_g(parts_g[0])
    query_a = gathered_a(parts_a[1])
    query_g = [gathered_g(part) for part in parts_g[1:]]

    order = jnp.concatenate([natural, me ^ jnp.array(order_mp, jnp.int32), home[None].astype(jnp.int32)])

    def eig_map(p, o):
        return (o[n_dp + p] * n_dp + o[n_dp + n_mp], 0)

    scaled, energy = scale(*train_a, train_g, (eigvals, eig_map), n_mp, order)
    total = scaled.shape[0]
    lanes = []
    for k in range(chunks):
        part = jnp.sum(score(*query_a, query_g[k], scaled, k, rows_q, order), axis=2)
        lanes.append(part.reshape(total, n_dp, rows_q // SEQ))
    part = jnp.concatenate(lanes, axis=2).reshape(total, -1)
    sums = jnp.concatenate([part, jnp.sum(energy, axis=(1, 2))[:, None]], axis=1)
    for axis, size in (("mp", n_mp), ("dp", n_dp)):
        bit = 1
        while bit < size:
            sums = sums + swap(sums, axis, size, bit)
            bit *= 2
    own = lax.dynamic_slice_in_dim(sums, home * (total // n_dp), total // n_dp, 0)
    scores = jnp.transpose(own[:, :-1]) * (1.0 / math.sqrt(features * hidden))
    energies = own[:, -1] / (features * hidden)
    return scores, energies


def solution(mesh):
    return jax.shard_map(
        functools.partial(on_device, mesh.shape["dp"], mesh.shape["mp"]),
        mesh=mesh,
        in_specs=(
            P("dp", "mp"),
            P("dp", "mp"),
            P("dp", "mp"),
            P("dp", "mp"),
            P("mp", None),
            P("mp", None),
            P(None, "mp"),
        ),
        out_specs=(P(None, "dp"), P("dp")),
        check_vma=False,
    )
```
